32 devices in a mesh: groups: 2 (over y), depth: 8 (over z, x), rows: 2 (over core).
Axes of the slice: x: 2, y: 2, z: 4, core: 2. Of those that a mesh axis runs over, the one named last changes fastest.
Arguments:
- samples: bfloat16 [16, 8, 2, 128, 128], P(('groups', 'depth'), None, 'rows'), parts along dimension 0, may hold values from -6 to 6
- spacing: float32 [16, 8, 2, 256], P(('groups', 'depth'), None, 'rows'), parts along dimension 0, may hold values from 0.025 to 0.5
- sample_counts: int32 [16, 8, 2, 1], P(('groups', 'depth'), None, 'rows'), parts along dimension 0, may hold values from 1 to 2, as said below
- directions: int32 [16, 2, 1], P('groups', 'rows'), parts along dimension 0, may hold values from 0 to 1
- w_first: bfloat16 [64, 128], replicated, may hold values from -0.75 to 0.75
- w_second: bfloat16 [128, 128], replicated, may hold values from -0.5 to 0.5
- w_out: bfloat16 [128, 17], replicated, may hold values from -0.5 to 0.5
- background: float32 [16], replicated, may hold values from -4 to 4
- dec_first: bfloat16 [64, 3, 3, 16], replicated, may hold values from -0.5 to 0.5
- dec_second: bfloat16 [64, 3, 3, 64], replicated, may hold values from -0.25 to 0.25
- dec_out: bfloat16 [3, 3, 3, 64], replicated, may hold values from -0.25 to 0.25
Outputs:
- rendered: float32 [32, 3, 128], P(('groups', 'depth', 'rows')), parts along dimension 0
The draws below stay inside these ranges and needn't reach their ends.
There are 2 independent parts, one for each index of `groups`. The reference program is written for one: setup_inputs(seed, part) draws one part's arguments, and reference() takes and returns one part's arrays. A program takes and returns all parts, laid end to end along the dimension named above; an argument that names none is the same for every part. Nothing has to cross between parts.
Inputs may be any that keep to these rules, and one draw needn't show every extreme that they name: `sample_counts`: slots at and past the count are padding; the count 2 is reached in every draw.
All inputs are finite; a program needn't handle non-finite values.
Results may differ from the reference program's by a relative error of at most 0.012.
Values may be sent and summed in bfloat16 or wider, within the bound.
A program may use at most 128 MiB of HBM per device.

```python
import math
import jax
import jax.numpy as jnp
from jax import lax

F_IN = 64
HID = 128
FEAT = 16
OUTS = 17
DEC = 64
COLORS = 3
K = 2
WIDTH = 128
BR = 1
SLABS = 8
BLOCKS = 8
BANDS = 2
HEIGHT = 16


def draw_sample_counts(key, part):
    shape = (SLABS, BLOCKS, BANDS, BR)
    key_counts = jax.random.fold_in(key, 11)
    key_spot = jax.random.fold_in(key, 23)
    counts = jax.random.randint(key_counts, shape, 1, K + 1).astype(jnp.int32)
    spot = jax.random.randint(key_spot, (), 0, SLABS * BLOCKS * BANDS * BR)
    flat = counts.reshape(-1).at[spot].set(K)
    return flat.reshape(shape).astype(jnp.int32)


def set_ends(values, rng, least, high):
    longest = values.shape.index(max(values.shape))
    spots = []
    for shift in (0, 1):
        where = [jax.random.randint(jax.random.fold_in(rng, axis), (), 0, length) for axis, length in enumerate(values.shape)]
        where[longest] = (where[longest] + shift) % values.shape[longest]
        spots.append(tuple(where))
    return values.at[spots[0]].set(least).at[spots[1]].set(high)


def levels(key, shape, cuts, low, high):
    gain = 1.0
    for position, parts in cuts:
        heights = jax.random.uniform(jax.random.fold_in(jax.random.fold_in(key, 6), position), (parts,), jnp.float32, low / len(cuts), high / len(cuts))
        gain = gain * jnp.repeat(jnp.exp(heights), shape[position] // parts).reshape((-1,) + (1,) * (len(shape) - 1 - position))
    return gain


def centred(own_key, dims, scale, reach, cuts=(), kind=jnp.bfloat16):
    array = jax.random.normal(own_key, dims, jnp.float32) * scale
    if len(cuts) > 0:
        array = levels(own_key, dims, cuts, -0.22, 0.18) * array
    return jnp.clip(array, min=-reach, max=reach).astype(kind)


def setup_inputs(seed: int = 0, part: int = 0) -> dict:
    splits = jax.random.split(jax.random.key(seed), 12)
    own_keys = jax.random.split(jax.random.fold_in(splits[11], part), 12)
    return {
        "samples": centred(own_keys[0], (SLABS, BLOCKS, BANDS, BR * WIDTH, K * F_IN), 1.0, 6.0, ((0, 8), (2, 2))),
        "spacing": jnp.clip(jnp.exp(math.log(0.5) - 2.9957323 * jax.random.uniform(own_keys[1], (SLABS, BLOCKS, BANDS, BR * WIDTH * K), jnp.float32) ** levels(own_keys[1], (SLABS, BLOCKS, BANDS, BR * WIDTH * K), ((0, 8), (2, 2)), -0.2, 0.2)), 0.025, 0.5),
        "sample_counts": draw_sample_counts(jax.random.fold_in(jax.random.fold_in(splits[11], part), 71), part),
        "directions": set_ends(jax.random.randint(own_keys[3], (BLOCKS, BANDS, BR), 0, 2), jax.random.fold_in(own_keys[3], 1), 0, 1).astype(jnp.int32),
        "w_first": centred(splits[4], (F_IN, HID), F_IN ** -0.5, 0.75),
        "w_second": centred(splits[5], (HID, HID), HID ** -0.5, 0.5),
        "w_out": centred(splits[6], (HID, OUTS), HID ** -0.5, 0.5),
        "background": centred(splits[7], (FEAT,), 1.0, 4.0, (), jnp.float32),
        "dec_first": centred(splits[8], (DEC, 3, 3, FEAT), (9 * FEAT) ** -0.5, 0.5),
        "dec_second": centred(splits[9], (DEC, 3, 3, DEC), (9 * DEC) ** -0.5, 0.25),
        "dec_out": centred(splits[10], (COLORS, 3, 3, DEC), (9 * DEC) ** -0.5, 0.25),
    }


def mlp_rows(inputs, w_first, w_second, w_out):
    hidden_one = jax.nn.silu(jnp.dot(inputs, w_first, preferred_element_type=jnp.float32)).astype(jnp.bfloat16)
    hidden_two = jax.nn.silu(jnp.dot(hidden_one, w_second, preferred_element_type=jnp.float32)).astype(jnp.bfloat16)
    return jnp.dot(hidden_two, w_out, preferred_element_type=jnp.float32)


def slab_partial(outputs, gaps, live):
    density = jax.nn.softplus(outputs[..., 0])
    opacity = 1.0 - jnp.exp(-density * gaps)
    passing = jnp.ones(live.shape, jnp.float32)
    color = jnp.zeros(live.shape + (outputs.shape[-1] - 1,), jnp.float32)
    for sample in range(outputs.shape[-2]):
        alpha = jnp.where(live > sample, opacity[..., sample], jnp.zeros_like(opacity[..., sample]))
        color = color + (passing * alpha)[..., None] * outputs[..., sample, 1:]
        passing = passing * (1.0 - alpha)
    return color, passing


def conv_image(field, weight):
    height = field.shape[0]
    cols = field.shape[2]
    padded = jnp.pad(field, ((1, 1), (0, 0), (1, 1)))
    taps = jnp.stack([padded[row_step:row_step + height, :, col_step:col_step + cols] for row_step in range(3) for col_step in range(3)], axis=1)
    taps = taps.reshape(height, -1, cols)
    kernel = weight.reshape(weight.shape[0], -1)
    return jnp.einsum('ok,rkw->row', kernel.astype(jnp.float32), taps.astype(jnp.float32))


def reference(samples, spacing, sample_counts, directions, w_first, w_second, w_out, background, dec_first, dec_second, dec_out):
    length = BR * WIDTH

    def one_slab(pieces):
        feats, gaps, counts = pieces
        outputs = mlp_rows(feats.reshape(-1, F_IN), w_first, w_second, w_out).reshape(BLOCKS, BANDS, length, K, FEAT + 1)
        live = jnp.broadcast_to(counts[..., None], (BLOCKS, BANDS, BR, WIDTH)).reshape(BLOCKS, BANDS, length)
        return slab_partial(outputs, gaps.reshape(BLOCKS, BANDS, length, K), live)

    colors, passes = lax.map(one_slab, (samples, spacing, sample_counts))

    def forward(carry, piece):
        acc_color, acc_pass = carry
        color, passing = piece
        return (acc_color + acc_pass[..., None] * color, acc_pass * passing), None

    start = (jnp.zeros((BLOCKS, BANDS, length, FEAT), jnp.float32), jnp.ones((BLOCKS, BANDS, length), jnp.float32))
    (front_color, total_pass), _ = lax.scan(forward, start, (colors, passes))
    (back_color, _), _ = lax.scan(forward, start, (colors, passes), reverse=True)
    ray_dirs = jnp.broadcast_to(directions[..., None], (BLOCKS, BANDS, BR, WIDTH)).reshape(BLOCKS, BANDS, length)
    color = jnp.where(ray_dirs[..., None] == 1, back_color, front_color)
    pixel = color + total_pass[..., None] * background
    image = pixel.reshape(HEIGHT, WIDTH, FEAT).transpose(0, 2, 1).astype(jnp.bfloat16)
    first = jax.nn.silu(conv_image(image, dec_first)).astype(jnp.bfloat16)
    second = jax.nn.silu(conv_image(first, dec_second)).astype(jnp.bfloat16)
    return conv_image(second, dec_out)
```

```python
import functools

import jax
import jax.numpy as jnp
from jax import lax
from jax.experimental import pallas as pl
from jax.experimental.pallas import tpu as pltpu
from jax.sharding import PartitionSpec as P

MESH = pl.DeviceIdType.MESH
HALO = 3
PAIR = 2
F32 = jnp.float32
BF16 = jnp.bfloat16


def silu(x):
    half = 0.5 * x
    return half + half * jnp.tanh(half)


def dot(a, b, dims=((1,), (0,)), precision=None):
    return lax.dot_general(a, b, (dims, ((), ())), precision=precision, preferred_element_type=F32)


def diagonal(block, slots):
    zero = jnp.zeros_like(block)
    return jnp.concatenate(
        [jnp.concatenate([block if i == j else zero for j in range(slots)], axis=1) for i in range(slots)],
        axis=0,
    )


def repeat(start, stop, body):
    if stop - start <= 8:
        for i in range(start, stop):
            body(i)
    else:
        def step(i, carry):
            body(i)
            return carry

        lax.fori_loop(start, stop, step, 0)


def pieces(v):
    high = v.astype(BF16)
    rest = v - high.astype(F32)
    mid = rest.astype(BF16)
    low = (rest - mid.astype(F32)).astype(BF16)
    return high, mid, low


def kernel(
    n,
    bands,
    slots,
    samples_hbm,
    spacing_hbm,
    counts_hbm,
    dirs_hbm,
    w1_hbm,
    w2_hbm,
    wo_hbm,
    bg_hbm,
    d1_hbm,
    d2_hbm,
    d3_hbm,
    out_ref,
    samples,
    spacing,
    counts,
    dirs,
    w1,
    w2,
    wo,
    bg,
    d1,
    d2,
    d3,
    gaps,
    part,
    recv,
    img,
    k2,
    k3,
    ray_sem,
    load_sem,
    send_sem,
    recv_sem,
    row_send,
    row_recv,
):
    depth = lax.axis_index("depth")
    band = lax.axis_index("rows")
    hub = bands - 1
    is_hub = band == hub
    me = depth * bands + band
    height = n * bands
    width = part.shape[3]
    feat = img.shape[1]
    hid = w2.shape[0]
    groups = n // PAIR
    plane = PAIR * bands
    mine = depth // PAIR
    spot = lax.rem(depth, PAIR) * bands + band
    span = PAIR * width
    late = mine >= groups // 2

    def order(k):
        return jnp.where(late, k, groups - 1 - k)

    def fetch(k):
        rows = pl.ds(pl.multiple_of(order(k) * span, span), span)
        return pltpu.make_async_copy(samples_hbm.at[rows], samples.at[rows], ray_sem.at[k])

    early = [(w1_hbm, w1), (spacing_hbm, spacing), (counts_hbm, counts), (dirs_hbm, dirs), (w2_hbm, w2), (wo_hbm, wo)]
    after = [(bg_hbm, bg), (d1_hbm, d1), (d2_hbm, d2), (d3_hbm, d3)]
    loads = [pltpu.make_async_copy(s, d, load_sem.at[i]) for i, (s, d) in enumerate(early + after)]
    loads[0].start()
    fetch(0).start()
    for load in loads[1 : len(early)]:
        load.start()
    repeat(1, groups, lambda k: fetch(k).start())

    barrier = pltpu.get_barrier_semaphore()

    def announce(where, core):
        pl.semaphore_signal(barrier, inc=1, device_id={"depth": where, "rows": core}, device_id_type=MESH)

    below = mine > 0
    above = mine < groups - 1

    @pl.when(is_hub)
    def _():
        def tell(i):
            up = i + (i >= depth).astype(jnp.int32)
            top = n - 1 - i
            down = top - (top <= depth).astype(jnp.int32)
            where = jnp.where(late, up, down)
            for core in range(bands):
                announce(where, core)

        repeat(0, n - 1, tell)
        for core in range(hub):
            announce(depth, core)

    @pl.when(jnp.logical_not(is_hub))
    def _():
        announce(depth, hub)

        @pl.when(jnp.logical_and(above, spot > 0))
        def _():
            announce(depth + PAIR, hub)

        @pl.when(jnp.logical_and(below, spot < plane - 1))
        def _():
            announce(depth - PAIR, hub)

    for load in loads[len(early) :]:
        load.start()

    home = lax.rem(depth, PAIR) * bands
    total = jnp.where(is_hub, n - 1 + hub, n)
    for core in range(hub):
        up = jnp.logical_and(above, home + core < plane - 1).astype(jnp.int32)
        down = jnp.logical_and(below, home + core > 0).astype(jnp.int32)
        total = total + jnp.where(is_hub, up + down, 0)

    src = lax.broadcasted_iota(jnp.int32, (slots * width, slots * width), 0)
    dst = lax.broadcasted_iota(jnp.int32, (slots * width, slots * width), 1)
    pick = (src == lax.rem(dst, width) * slots + dst // width).astype(F32).astype(BF16)
    for load in loads[1:4]:
        load.wait()

    def column(v, rows):
        row_id = lax.broadcasted_iota(jnp.int32, (rows, n), 0)
        col_id = lax.broadcasted_iota(jnp.int32, (rows, n), 1)
        return lambda base: jnp.sum(jnp.where(row_id + base == col_id, v, 0.0), axis=1, keepdims=True)

    step = 8 if n % 8 == 0 else n
    count_of = column(counts[...].astype(F32), step)
    dir_of = column(dirs[...].astype(F32), step)
    for base in range(0, n, step):
        lines = jnp.concatenate(
            [spacing[pl.ds(base * slots + j, step, stride=slots), :] for j in range(slots)], axis=1
        )
        high, mid, low = pieces(lines)
        flat = dot(jnp.concatenate([high, mid, low], axis=0), pick)
        flat = flat[:step] + flat[step : 2 * step] + flat[2 * step :]
        count = count_of(base)
        falls = jnp.broadcast_to(dir_of(base), (step, width))
        for s in range(slots):
            kept = jnp.where(count > float(s), flat[:, s * width : (s + 1) * width], 0.0)
            for i in range(step):
                gaps[base + i, s : s + 1, :] = kept[i : i + 1, :]
        for i in range(step):
            gaps[base + i, slots : slots + 1, :] = falls[i : i + 1, :]

    loads[0].wait()
    w1d = diagonal(w1[...], slots)
    for load in loads[4 : len(early)]:
        load.wait()
    w2d = diagonal(w2[...], slots)
    wo_all = wo[...].astype(F32)
    feat_w = wo_all[1:, :].astype(BF16)
    dens_w = wo_all[:1, :]
    zero_f = jnp.zeros_like(feat_w)
    zero_d = jnp.zeros_like(dens_w)
    feat_rows = [
        jnp.concatenate([feat_w if i == j else zero_f for j in range(slots)], axis=1) for i in range(slots)
    ]
    dens_rows = [
        jnp.concatenate([dens_w if i == j else zero_d for j in range(slots)], axis=1) for i in range(slots)
    ]
    pad = jnp.zeros((16 - slots, slots * hid), F32)
    tail = jnp.concatenate(dens_rows + [pad], axis=0).astype(BF16)
    wod = jnp.concatenate(feat_rows + [tail], axis=0)

    def compute(k):
        q = order(k)
        fetch(k).wait()
        rays = samples[pl.ds(pl.multiple_of(q * span, span), span), :]
        one = silu(dot(rays, w1d)).astype(BF16)
        two = silu(dot(one, w2d)).astype(BF16)
        out = dot(wod, two, ((1,), (1,)))
        held = [gaps[q * PAIR + i] for i in range(PAIR)]
        gap = jnp.concatenate([h[:slots] for h in held], axis=1)
        logit = out[slots * feat : slots * feat + slots, :]
        density = jnp.maximum(logit, 0.0) + jnp.log1p(jnp.exp(-jnp.abs(logit)))
        clear = jnp.exp(-density * gap)
        alpha = 1.0 - clear
        color = jnp.zeros((feat, span), F32)
        passing = jnp.ones((1, span), F32)
        for s in range(slots):
            color = color + (passing * alpha[s : s + 1, :]) * out[s * feat : (s + 1) * feat, :]
            passing = passing * clear[s : s + 1, :]
        high = passing.astype(BF16).astype(F32)
        zeros = jnp.zeros((5, width), F32)
        for i in range(PAIR):
            at = slice(i * width, (i + 1) * width)
            part[q, i, :feat, :] = color[:, at].astype(BF16)
            part[q, i, feat:, :] = jnp.concatenate(
                [high[:, at], passing[:, at] - high[:, at], held[i][slots:], zeros], axis=0
            ).astype(BF16)

    slot = band * n + depth
    msgs = bands * n

    def slab_copy(q, where):
        return pltpu.make_async_remote_copy(
            src_ref=part.at[q],
            dst_ref=recv.at[slot],
            send_sem=send_sem,
            recv_sem=recv_sem,
            device_id={"depth": where, "rows": hub},
            device_id_type=MESH,
        )

    def send(k):
        q = order(k)
        for x in range(PAIR):
            where = q * PAIR + x
            local = jnp.logical_and(where == depth, is_hub)

            @pl.when(jnp.logical_not(local))
            def _(where=where):
                slab_copy(q, where).start()

            @pl.when(local)
            def _():
                recv[slot] = part[q]

    def stage(k):
        compute(k)
        if isinstance(k, int):
            if k == 0:
                pl.semaphore_wait(barrier, total)
        else:
            @pl.when(k == 0)
            def _():
                pl.semaphore_wait(barrier, total)
        send(k)

    repeat(0, groups, stage)

    for load in loads[len(early) :]:
        load.wait()
    out_ch = d2.shape[2]
    mid_ch = d2.shape[3]
    colors = d3.shape[0]
    eye = (
        lax.broadcasted_iota(jnp.int32, (out_ch, out_ch), 0)
        == lax.broadcasted_iota(jnp.int32, (out_ch, out_ch), 1)
    ).astype(BF16)
    k1 = dot(eye, d1[...], ((1,), (1,))).astype(BF16)
    k3[...] = jnp.zeros_like(k3)
    for a in range(3):
        for b in range(3):
            k2[b * out_ch : (b + 1) * out_ch, a * mid_ch : (a + 1) * mid_ch] = d2[a, b]
    for o in range(colors):
        for a in range(3):
            tile = d3[o, a].astype(F32)
            for b in range(3):
                k3[b * 8 + o : b * 8 + o + 1, a * mid_ch : (a + 1) * mid_ch] = tile[b : b + 1, :]
    sq = (
        lax.broadcasted_iota(jnp.int32, (feat, feat), 0)
        == lax.broadcasted_iota(jnp.int32, (feat, feat), 1)
    )
    bg_col = jnp.sum(jnp.where(sq, bg[...], 0.0), axis=1, keepdims=True)

    @pl.when(jnp.logical_not(below))
    def _():
        img[:HALO] = jnp.zeros((HALO,) + img.shape[1:], BF16)

    @pl.when(jnp.logical_not(above))
    def _():
        img[HALO + plane :] = jnp.zeros((HALO,) + img.shape[1:], BF16)

    def row_copy(first, landing, sem, where, core):
        rows = plane if sem == 0 else HALO
        return pltpu.make_async_remote_copy(
            src_ref=img.at[pl.ds(first, rows)],
            dst_ref=img.at[pl.ds(landing, rows)],
            send_sem=row_send.at[sem * bands + core],
            recv_sem=row_recv.at[sem],
            device_id={"depth": where, "rows": core},
            device_id_type=MESH,
        )

    def to_core(core):
        return row_copy(HALO, HALO, 0, depth, core)

    def to_above(core):
        return row_copy(plane, 0, 1, depth + PAIR, core)

    def to_below(core):
        return row_copy(HALO, HALO + plane, 2, depth - PAIR, core)

    def outgoing(act):
        for core in range(hub):
            act(to_core(core))
        for core in range(bands):
            @pl.when(jnp.logical_and(above, home + core < plane - 1))
            def _(core=core):
                act(to_above(core))

            @pl.when(jnp.logical_and(below, home + core > 0))
            def _(core=core):
                act(to_below(core))

    @pl.when(is_hub)
    def _():
        bulk = recv.at[pl.ds(0, msgs - 1)]
        pltpu.make_async_copy(bulk, bulk, recv_sem).wait()
        for i in range(PAIR):
            for b in range(bands):
                def fold(s, carry):
                    rise, light, fall = carry
                    message = recv[b * n + s, i].astype(F32)
                    color = message[:feat]
                    passing = message[feat : feat + 1] + message[feat + 1 : feat + 2]
                    return rise + light * color, light * passing, color + passing * fall

                carry = (
                    jnp.zeros((feat, width), F32),
                    jnp.ones((1, width), F32),
                    jnp.zeros((feat, width), F32),
                )
                if n <= 8:
                    for s in range(n):
                        carry = fold(s, carry)
                else:
                    carry = lax.fori_loop(0, n, fold, carry)
                rise, light, fall = carry
                falling = recv[b * n, i].astype(F32)[feat + 2 : feat + 3] > 0.5
                pixel = jnp.where(falling, fall, rise) + light * bg_col
                img[HALO + i * bands + b] = pixel.astype(BF16)
        outgoing(lambda copy: copy.start())

    lane = lax.broadcasted_iota(jnp.int32, (1, width), 1)

    def left_of(v):
        return jnp.where(lane == 0, 0.0, pltpu.roll(v, 1, 1))

    def right_of(v):
        return jnp.where(lane == width - 1, 0.0, pltpu.roll(v, width - 1, 1))

    def columns(v):
        return jnp.concatenate([left_of(v).astype(BF16), v.astype(BF16), right_of(v).astype(BF16)], axis=0)

    @pl.when(jnp.logical_not(is_hub))
    def _():
        to_core(0).wait_recv()

    @pl.when(jnp.logical_and(below, spot < plane - 1))
    def _():
        to_above(0).wait_recv()

    @pl.when(jnp.logical_and(above, spot > 0))
    def _():
        to_below(0).wait_recv()

    def inside(v, offset):
        row = me + offset
        ok = jnp.logical_and(row >= 0, row < height)
        return jnp.where(ok, v, 0.0)

    def stacked(rows):
        return jnp.concatenate(
            [jnp.concatenate(rows[j : j + 3], axis=0) for j in range(len(rows) - 2)], axis=1
        )

    first = silu(dot(k1, stacked([columns(img[spot + j].astype(F32)) for j in range(2 * HALO + 1)])))
    first = [inside(first[:, j * width : (j + 1) * width], j - 2).astype(BF16) for j in range(5)]
    wide = dot(k2[...], stacked(first))
    second = []
    for j in range(3):
        at = slice(j * width, (j + 1) * width)
        taps = [wide[b * out_ch : (b + 1) * out_ch, at] for b in range(3)]
        second.append(inside(silu(left_of(taps[0]) + taps[1] + right_of(taps[2])), j - 1).astype(BF16))
    taps = dot(k3[...].astype(BF16), stacked(second))
    final = left_of(taps[:8]) + taps[8:16] + right_of(taps[16:24])
    for o in range(colors):
        out_ref[o] = final[o : o + 1, :]


    @pl.when(is_hub)
    def _():
        bulk = recv.at[pl.ds(0, n - 1)]
        pltpu.make_async_copy(bulk, bulk, send_sem).wait()
        outgoing(lambda copy: copy.wait_send())

    @pl.when(jnp.logical_not(is_hub))
    def _():
        bulk = recv.at[pl.ds(0, n)]
        pltpu.make_async_copy(bulk, bulk, send_sem).wait()


def shards(
    samples, spacing, sample_counts, directions, w_first, w_second, w_out, background, dec_first, dec_second, dec_out
):
    feat_in, hid = w_first.shape
    n = samples.shape[1]
    width = samples.shape[3]
    slots = samples.shape[4] // feat_in
    feat = w_out.shape[1] - 1
    bands = lax.axis_size("rows")
    assert n == lax.axis_size("depth") and sample_counts.shape[3] == 1 and n % PAIR == 0 and bands == 2
    colors = dec_out.shape[0]
    mid = dec_second.shape[0]
    args = (
        samples.reshape(n * width, slots * feat_in),
        spacing.reshape(n * slots, width),
        sample_counts.reshape(1, n),
        directions.reshape(1, n),
        w_first,
        w_second,
        w_out.T,
        background.reshape(1, feat),
        dec_first.transpose(1, 2, 3, 0).reshape(9 * feat, mid),
        dec_second.transpose(1, 2, 0, 3),
        dec_out,
    )
    rows = feat + 8
    out = pl.pallas_call(
        functools.partial(kernel, n, bands, slots),
        out_shape=pltpu.VMEM((colors, 1, width), F32),
        in_specs=[pl.BlockSpec(memory_space=pl.ANY)] * len(args),
        out_specs=pl.BlockSpec(memory_space=pltpu.VMEM),
        scratch_shapes=[pltpu.VMEM(a.shape, a.dtype) for a in args]
        + [
            pltpu.VMEM((n, slots + 1, width), F32),
            pltpu.VMEM((n // PAIR, PAIR, rows, width), BF16),
            pltpu.VMEM((bands * n, PAIR, rows, width), BF16),
            pltpu.VMEM((2 * HALO + PAIR * bands, feat, width), BF16),
            pltpu.VMEM((3 * mid, 3 * mid), BF16),
            pltpu.VMEM((24, 3 * mid), F32),
            pltpu.SemaphoreType.DMA((n // PAIR,)),
            pltpu.SemaphoreType.DMA((len(args) - 1,)),
            pltpu.SemaphoreType.DMA,
            pltpu.SemaphoreType.DMA,
            pltpu.SemaphoreType.DMA((3 * bands,)),
            pltpu.SemaphoreType.DMA((3,)),
        ],
        compiler_params=pltpu.CompilerParams(collective_id=0, has_side_effects=True),
    )(*args)
    return out.transpose(1, 0, 2)


def solution(mesh):
    in_specs = (
        P(("groups", "depth"), None, "rows", None, None),
        P(("groups", "depth"), None, "rows", None),
        P(("groups", "depth"), None, "rows", None),
        P("groups", "rows", None),
        P(),
        P(),
        P(),
        P(),
        P(),
        P(),
        P(),
    )
    out_specs = P(("groups", "depth", "rows"), None, None)
    return jax.shard_map(shards, mesh=mesh, in_specs=in_specs, out_specs=out_specs, check_vma=False)
```

```python
import functools

import jax
import jax.numpy as jnp
from jax import lax
from jax.experimental import pallas as pl
from jax.experimental.pallas import tpu as pltpu
from jax.sharding import PartitionSpec as P

MESH = pl.DeviceIdType.MESH
HALO = 3
PAIR = 2
F32 = jnp.float32
BF16 = jnp.bfloat16


def silu(x):
    half = 0.5 * x
    return half + half * jnp.tanh(half)


def dot(a, b, dims=((1,), (0,)), precision=None):
    return lax.dot_general(a, b, (dims, ((), ())), precision=precision, preferred_element_type=F32)


def diagonal(block, slots):
    zero = jnp.zeros_like(block)
    return jnp.concatenate(
        [jnp.concatenate([block if i == j else zero for j in range(slots)], axis=1) for i in range(slots)],
        axis=0,
    )


def repeat(start, stop, body):
    if stop - start <= 8:
        for i in range(start, stop):
            body(i)
    else:
        def step(i, carry):
            body(i)
            return carry

        lax.fori_loop(start, stop, step, 0)


def pieces(v):
    high = v.astype(BF16)
    rest = v - high.astype(F32)
    mid = rest.astype(BF16)
    low = (rest - mid.astype(F32)).astype(BF16)
    return high, mid, low


def kernel(
    n,
    bands,
    slots,
    samples_hbm,
    spacing_hbm,
    counts_hbm,
    dirs_hbm,
    w1_hbm,
    w2_hbm,
    wo_hbm,
    bg_hbm,
    d1_hbm,
    d2_hbm,
    d3_hbm,
    out_ref,
    samples,
    spacing,
    counts,
    dirs,
    w1,
    w2,
    wo,
    bg,
    d1,
    d2,
    d3,
    gaps,
    part,
    recv,
    img,
    k2,
    k3,
    ray_sem,
    load_sem,
    send_sem,
    recv_sem,
    row_send,
    row_recv,
):
    depth = lax.axis_index("depth")
    band = lax.axis_index("rows")
    hub = bands - 1
    is_hub = band == hub
    me = depth * bands + band
    height = n * bands
    width = part.shape[3]
    feat = img.shape[1]
    hid = w2.shape[0]
    groups = n // PAIR
    plane = PAIR * bands
    mine = depth // PAIR
    spot = lax.rem(depth, PAIR) * bands + band
    span = PAIR * width
    half = groups // 2
    late = mine >= half

    def fetch(k):
        rows = pl.ds(k * span, span)
        return pltpu.make_async_copy(samples_hbm.at[rows], samples.at[rows], ray_sem.at[k])

    early = [(w1_hbm, w1), (spacing_hbm, spacing), (counts_hbm, counts), (dirs_hbm, dirs), (w2_hbm, w2), (wo_hbm, wo)]
    after = [(bg_hbm, bg), (d1_hbm, d1), (d2_hbm, d2), (d3_hbm, d3)]
    loads = [pltpu.make_async_copy(s, d, load_sem.at[i]) for i, (s, d) in enumerate(early + after)]
    loads[0].start()
    fetch(0).start()
    for load in loads[1 : len(early)]:
        load.start()
    repeat(1, groups, lambda k: fetch(k).start())

    barrier = pltpu.get_barrier_semaphore()

    def announce(where, core):
        pl.semaphore_signal(barrier, inc=1, device_id={"depth": where, "rows": core}, device_id_type=MESH)

    below = mine > 0
    above = mine < groups - 1

    soon = jnp.logical_not(late)

    @pl.when(is_hub)
    def _():
        def tell(i):
            where = i + (i >= depth).astype(jnp.int32)
            for core in range(bands):
                announce(where, core)

        repeat(0, n - 1, tell)
        for core in range(hub):
            announce(depth, core)

    @pl.when(jnp.logical_not(is_hub))
    def _():
        announce(depth, hub)

        @pl.when(jnp.logical_and(above, spot > 0))
        def _():
            announce(depth + PAIR, hub)

        @pl.when(jnp.logical_and(below, spot < plane - 1))
        def _():
            announce(depth - PAIR, hub)

    for load in loads[len(early) :]:
        load.start()

    home = lax.rem(depth, PAIR) * bands
    total = jnp.where(is_hub, n - 1 + hub, n)
    for core in range(hub):
        up = jnp.logical_and(above, home + core < plane - 1).astype(jnp.int32)
        down = jnp.logical_and(below, home + core > 0).astype(jnp.int32)
        total = total + jnp.where(is_hub, up + down, 0)

    src = lax.broadcasted_iota(jnp.int32, (slots * width, slots * width), 0)
    dst = lax.broadcasted_iota(jnp.int32, (slots * width, slots * width), 1)
    pick = (src == lax.rem(dst, width) * slots + dst // width).astype(F32).astype(BF16)
    for load in loads[1:4]:
        load.wait()

    def column(v, rows):
        row_id = lax.broadcasted_iota(jnp.int32, (rows, n), 0)
        col_id = lax.broadcasted_iota(jnp.int32, (rows, n), 1)
        return lambda base: jnp.sum(jnp.where(row_id + base == col_id, v, 0.0), axis=1, keepdims=True)

    step = 8 if n % 8 == 0 else n
    count_of = column(counts[...].astype(F32), step)
    dir_of = column(dirs[...].astype(F32), step)
    for base in range(0, n, step):
        lines = jnp.concatenate(
            [spacing[pl.ds(base * slots + j, step, stride=slots), :] for j in range(slots)], axis=1
        )
        high, mid, low = pieces(lines)
        flat = dot(jnp.concatenate([high, mid, low], axis=0), pick)
        flat = flat[:step] + flat[step : 2 * step] + flat[2 * step :]
        count = count_of(base)
        falls = jnp.broadcast_to(dir_of(base), (step, width))
        for s in range(slots):
            kept = jnp.where(count > float(s), flat[:, s * width : (s + 1) * width], 0.0)
            for i in range(step):
                gaps[base + i, s : s + 1, :] = kept[i : i + 1, :]
        for i in range(step):
            gaps[base + i, slots : slots + 1, :] = falls[i : i + 1, :]

    loads[0].wait()
    w1d = diagonal(w1[...], slots)
    for load in loads[4 : len(early)]:
        load.wait()
    w2d = diagonal(w2[...], slots)
    wo_all = wo[...].astype(F32)
    feat_w = wo_all[1:, :].astype(BF16)
    dens_w = wo_all[:1, :]
    zero_f = jnp.zeros_like(feat_w)
    zero_d = jnp.zeros_like(dens_w)
    feat_rows = [
        jnp.concatenate([feat_w if i == j else zero_f for j in range(slots)], axis=1) for i in range(slots)
    ]
    dens_rows = [
        jnp.concatenate([dens_w if i == j else zero_d for j in range(slots)], axis=1) for i in range(slots)
    ]
    pad = jnp.zeros((16 - slots, slots * hid), F32)
    tail = jnp.concatenate(dens_rows + [pad], axis=0).astype(BF16)
    wod = jnp.concatenate(feat_rows + [tail], axis=0)

    def compute(k):
        q = k
        fetch(k).wait()
        rays = samples[pl.ds(q * span, span), :]
        one = silu(dot(rays, w1d)).astype(BF16)
        two = silu(dot(one, w2d)).astype(BF16)
        out = dot(wod, two, ((1,), (1,)))
        held = [gaps[q * PAIR + i] for i in range(PAIR)]
        gap = jnp.concatenate([h[:slots] for h in held], axis=1)
        logit = out[slots * feat : slots * feat + slots, :]
        density = jnp.maximum(logit, 0.0) + jnp.log1p(jnp.exp(-jnp.abs(logit)))
        clear = jnp.exp(-density * gap)
        alpha = 1.0 - clear
        color = jnp.zeros((feat, span), F32)
        passing = jnp.ones((1, span), F32)
        for s in range(slots):
            color = color + (passing * alpha[s : s + 1, :]) * out[s * feat : (s + 1) * feat, :]
            passing = passing * clear[s : s + 1, :]
        for i in range(PAIR):
            at = slice(i * width, (i + 1) * width)
            part[q, i, :feat, :] = color[:, at].astype(BF16)
            mark = passing[:, at] + 4.0 * held[i][slots:]
            high = mark.astype(BF16).astype(F32)
            part[q, i, feat:, :] = jnp.concatenate([high, mark - high], axis=0).astype(BF16)

    slot = band * n + depth
    msgs = bands * n

    def slab_copy(q, where):
        return pltpu.make_async_remote_copy(
            src_ref=part.at[q],
            dst_ref=recv.at[slot],
            send_sem=send_sem,
            recv_sem=recv_sem,
            device_id={"depth": where, "rows": hub},
            device_id_type=MESH,
        )

    def send(q):
        for x in range(PAIR):
            where = q * PAIR + x
            local = jnp.logical_and(where == depth, is_hub)

            @pl.when(jnp.logical_not(local))
            def _(where=where):
                slab_copy(q, where).start()

            @pl.when(local)
            def _():
                recv[slot] = part[q]

    def stage(k):
        compute(k)

        @pl.when(late)
        def _():
            if isinstance(k, int):
                if k == 0:
                    pl.semaphore_wait(barrier, total)
            else:
                @pl.when(k == 0)
                def _():
                    pl.semaphore_wait(barrier, total)
            send(k)

    repeat(0, groups, stage)

    for load in loads[len(early) :]:
        load.wait()
    out_ch = d2.shape[2]
    mid_ch = d2.shape[3]
    colors = d3.shape[0]
    eye = (
        lax.broadcasted_iota(jnp.int32, (out_ch, out_ch), 0)
        == lax.broadcasted_iota(jnp.int32, (out_ch, out_ch), 1)
    ).astype(BF16)
    k1 = dot(eye, d1[...], ((1,), (1,))).astype(BF16)
    k3[...] = jnp.zeros_like(k3)
    for a in range(3):
        for b in range(3):
            k2[b * out_ch : (b + 1) * out_ch, a * mid_ch : (a + 1) * mid_ch] = d2[a, b]
    for o in range(colors):
        for a in range(3):
            tile = d3[o, a].astype(F32)
            for b in range(3):
                k3[b * 8 + o : b * 8 + o + 1, a * mid_ch : (a + 1) * mid_ch] = tile[b : b + 1, :]
    sq = (
        lax.broadcasted_iota(jnp.int32, (feat, feat), 0)
        == lax.broadcasted_iota(jnp.int32, (feat, feat), 1)
    )
    bg_col = jnp.sum(jnp.where(sq, bg[...], 0.0), axis=1, keepdims=True)

    @pl.when(jnp.logical_not(below))
    def _():
        img[:HALO] = jnp.zeros((HALO,) + img.shape[1:], BF16)

    @pl.when(jnp.logical_not(above))
    def _():
        img[HALO + plane :] = jnp.zeros((HALO,) + img.shape[1:], BF16)

    @pl.when(soon)
    def _():
        pl.semaphore_wait(barrier, total)
        repeat(0, groups, send)

    def row_copy(first, landing, sem, where, core):
        rows = plane if sem == 0 else HALO
        return pltpu.make_async_remote_copy(
            src_ref=img.at[pl.ds(first, rows)],
            dst_ref=img.at[pl.ds(landing, rows)],
            send_sem=row_send.at[sem * bands + core],
            recv_sem=row_recv.at[sem],
            device_id={"depth": where, "rows": core},
            device_id_type=MESH,
        )

    def to_core(core):
        return row_copy(HALO, HALO, 0, depth, core)

    def to_above(core):
        return row_copy(plane, 0, 1, depth + PAIR, core)

    def to_below(core):
        return row_copy(HALO, HALO + plane, 2, depth - PAIR, core)

    def outgoing(act):
        for core in range(hub):
            act(to_core(core))
        for core in range(bands):
            @pl.when(jnp.logical_and(above, home + core < plane - 1))
            def _(core=core):
                act(to_above(core))

            @pl.when(jnp.logical_and(below, home + core > 0))
            def _(core=core):
                act(to_below(core))

    @pl.when(is_hub)
    def _():
        bulk = recv.at[pl.ds(0, msgs - 1)]
        pltpu.make_async_copy(bulk, bulk, recv_sem).wait()
        for i in range(PAIR):
            for b in range(bands):
                def fold(s, carry):
                    rise, light, fall = carry
                    message = recv[b * n + s, i].astype(F32)
                    color = message[:feat]
                    mark = message[feat : feat + 1] + message[feat + 1 : feat + 2]
                    passing = jnp.where(mark > 2.0, mark - 4.0, mark)
                    return rise + light * color, light * passing, color + passing * fall

                carry = (
                    jnp.zeros((feat, width), F32),
                    jnp.ones((1, width), F32),
                    jnp.zeros((feat, width), F32),
                )
                if n <= 8:
                    for s in range(n):
                        carry = fold(s, carry)
                else:
                    carry = lax.fori_loop(0, n, fold, carry)
                rise, light, fall = carry
                falling = recv[b * n, i].astype(F32)[feat : feat + 1] > 2.0
                pixel = jnp.where(falling, fall, rise) + light * bg_col
                img[HALO + i * bands + b] = pixel.astype(BF16)
        outgoing(lambda copy: copy.start())

    lane = lax.broadcasted_iota(jnp.int32, (1, width), 1)

    def left_of(v):
        return jnp.where(lane == 0, 0.0, pltpu.roll(v, 1, 1))

    def right_of(v):
        return jnp.where(lane == width - 1, 0.0, pltpu.roll(v, width - 1, 1))

    def columns(v):
        return jnp.concatenate([left_of(v).astype(BF16), v.astype(BF16), right_of(v).astype(BF16)], axis=0)

    @pl.when(jnp.logical_not(is_hub))
    def _():
        to_core(0).wait_recv()

    @pl.when(jnp.logical_and(below, spot < plane - 1))
    def _():
        to_above(0).wait_recv()

    @pl.when(jnp.logical_and(above, spot > 0))
    def _():
        to_below(0).wait_recv()

    def inside(v, offset):
        row = me + offset
        ok = jnp.logical_and(row >= 0, row < height)
        return jnp.where(ok, v, 0.0)

    def stacked(rows):
        return jnp.concatenate(
            [jnp.concatenate(rows[j : j + 3], axis=0) for j in range(len(rows) - 2)], axis=1
        )

    first = silu(dot(k1, stacked([columns(img[spot + j].astype(F32)) for j in range(2 * HALO + 1)])))
    first = [inside(first[:, j * width : (j + 1) * width], j - 2).astype(BF16) for j in range(5)]
    wide = dot(k2[...], stacked(first))
    second = []
    for j in range(3):
        at = slice(j * width, (j + 1) * width)
        taps = [wide[b * out_ch : (b + 1) * out_ch, at] for b in range(3)]
        second.append(inside(silu(left_of(taps[0]) + taps[1] + right_of(taps[2])), j - 1).astype(BF16))
    taps = dot(k3[...].astype(BF16), stacked(second))
    final = left_of(taps[:8]) + taps[8:16] + right_of(taps[16:24])
    for o in range(colors):
        out_ref[o] = final[o : o + 1, :]


    @pl.when(is_hub)
    def _():
        bulk = recv.at[pl.ds(0, n - 1)]
        pltpu.make_async_copy(bulk, bulk, send_sem).wait()
        outgoing(lambda copy: copy.wait_send())

    @pl.when(jnp.logical_not(is_hub))
    def _():
        bulk = recv.at[pl.ds(0, n)]
        pltpu.make_async_copy(bulk, bulk, send_sem).wait()


def shards(
    samples, spacing, sample_counts, directions, w_first, w_second, w_out, background, dec_first, dec_second, dec_out
):
    feat_in, hid = w_first.shape
    n = samples.shape[1]
    width = samples.shape[3]
    slots = samples.shape[4] // feat_in
    feat = w_out.shape[1] - 1
    bands = lax.axis_size("rows")
    assert n == lax.axis_size("depth") and sample_counts.shape[3] == 1 and n % (2 * PAIR) == 0 and bands == 2
    colors = dec_out.shape[0]
    mid = dec_second.shape[0]
    args = (
        samples.reshape(n * width, slots * feat_in),
        spacing.reshape(n * slots, width),
        sample_counts.reshape(1, n),
        directions.reshape(1, n),
        w_first,
        w_second,
        w_out.T,
        background.reshape(1, feat),
        dec_first.transpose(1, 2, 3, 0).reshape(9 * feat, mid),
        dec_second.transpose(1, 2, 0, 3),
        dec_out,
    )
    rows = feat + 2
    out = pl.pallas_call(
        functools.partial(kernel, n, bands, slots),
        out_shape=pltpu.VMEM((colors, 1, width), F32),
        in_specs=[pl.BlockSpec(memory_space=pl.ANY)] * len(args),
        out_specs=pl.BlockSpec(memory_space=pltpu.VMEM),
        scratch_shapes=[pltpu.VMEM(a.shape, a.dtype) for a in args]
        + [
            pltpu.VMEM((n, slots + 1, width), F32),
            pltpu.VMEM((n // PAIR, PAIR, rows, width), BF16),
            pltpu.VMEM((bands * n, PAIR, rows, width), BF16),
            pltpu.VMEM((2 * HALO + PAIR * bands, feat, width), BF16),
            pltpu.VMEM((3 * mid, 3 * mid), BF16),
            pltpu.VMEM((24, 3 * mid), F32),
            pltpu.SemaphoreType.DMA((n // PAIR,)),
            pltpu.SemaphoreType.DMA((len(args) - 1,)),
            pltpu.SemaphoreType.DMA,
            pltpu.SemaphoreType.DMA,
            pltpu.SemaphoreType.DMA((3 * bands,)),
            pltpu.SemaphoreType.DMA((3,)),
        ],
        compiler_params=pltpu.CompilerParams(collective_id=0, has_side_effects=True),
    )(*args)
    return out.transpose(1, 0, 2)


def solution(mesh):
    in_specs = (
        P(("groups", "depth"), None, "rows", None, None),
        P(("groups", "depth"), None, "rows", None),
        P(("groups", "depth"), None, "rows", None),
        P("groups", "rows", None),
        P(),
        P(),
        P(),
        P(),
        P(),
        P(),
        P(),
    )
    out_specs = P(("groups", "depth", "rows"), None, None)
    return jax.shard_map(shards, mesh=mesh, in_specs=in_specs, out_specs=out_specs, check_vma=False)
```
